256 devices in a mesh: grid: 8 (over x_lo, y), dom: 32 (over z, x_hi, core).
Axes of the slice: x: 4 (x_hi: 2, x_lo: 2; x = x_hi * 2 + x_lo), y: 4, z: 8, core: 2. Of those that a mesh axis runs over, the one named last changes fastest.
Arguments:
- state_field: float32 [8, 64, 8, 16384], P('grid', 'dom'), may hold values from -6 to 6
- level_vectors: int32 [8, 4], P('grid'), may hold values from 2 to 5, as said below
- combine_weights: int32 [8], P('grid'), may hold values from -2 to 2, as said below
- diffusion: float32 [6], replicated, may hold values from 0.05 to 0.08
- courant: float32 [6], replicated, may hold values from -0.3 to 0.3
Outputs:
- combined_field: float32 [8, 64, 8, 16384], P('grid', 'dom')
The draws below stay inside these ranges and needn't reach their ends.
Inputs may be any that keep to these rules, and one draw needn't show every extreme that they name: `level_vectors`: each row holds 2, 3, 4, 5 in some order. `combine_weights`: never zero.
All inputs are finite; a program needn't handle non-finite values.
Results may differ from the reference program's by a relative error of at most 0.0003.
Values sent between devices are 32-bit elements; how exact they have to be, the bound alone decides.
No kernel may reach another device: no remote copies, remote signals or barrier semaphores. Data moves between devices by JAX's collectives and lax.ppermute only.
A program may use at most 128 MiB of HBM per device.

```python
import jax
import jax.numpy as jnp
from jax import lax

SECOND = 8
LOW = 2
LOCAL = 16384
NX = 64
GRIDS = 8


def draw_level_vectors(key, part):
    scores = jax.random.randint(jax.random.fold_in(key, 11), (GRIDS, 4), 0, 1024) * 4 + jnp.arange(4, dtype=jnp.int32)[None, :]
    ordering = jnp.argsort(scores, axis=1, stable=True).astype(jnp.int32)
    return (ordering + LOW).astype(jnp.int32)


def draw_combine_weights(key, part):
    picks = jax.random.randint(jax.random.fold_in(key, 23), (GRIDS,), 0, 4)
    return (picks - 2 + (picks >= 2).astype(jnp.int32)).astype(jnp.int32)


def level_of(own_key, shape, split, smallest, top_value):
    def one(position, blocks):
        steps = jax.random.uniform(jax.random.fold_in(jax.random.fold_in(own_key, 6), position), (blocks,), jnp.float32, smallest / len(split), top_value / len(split))
        return jnp.repeat(jnp.exp(steps), shape[position] // blocks).reshape((-1,) + (1,) * (len(shape) - position - 1))

    loudness = one(*split[0])
    for cut in split[1:]:
        loudness = loudness * one(*cut)
    return loudness


def bell_draw(rng, dims, deviation, bound, shards=(), kind=jnp.bfloat16):
    drawn = deviation * jax.random.normal(rng, dims, jnp.float32)
    if shards:
        drawn = drawn * level_of(rng, dims, shards, -0.22, 0.18)
    return jnp.clip(drawn, -bound, bound).astype(kind)


def setup_inputs(seed: int = 0) -> dict:
    keys = jax.random.split(jax.random.key(seed), 6)
    state_field = bell_draw(keys[0], (GRIDS, NX, SECOND, LOCAL), 1.0, 6.0, ((0, 8), (1, 32)), jnp.float32)
    level_vectors = draw_level_vectors(jax.random.fold_in(keys[5], 71), 0)
    combine_weights = draw_combine_weights(jax.random.fold_in(keys[5], 71), 0)
    diffusion = jnp.clip(jax.random.uniform(keys[3], (6,), jnp.float32, 0.05, 0.08), 0.05, 0.08)
    courant = jnp.clip(jax.random.uniform(keys[4], (6,), jnp.float32, -0.3, 0.3), -0.3, 0.3)
    return dict(state_field=state_field, level_vectors=level_vectors, combine_weights=combine_weights, diffusion=diffusion, courant=courant)


def level_pass(values, dimension, spacing, orientation):
    length = values.shape[dimension]
    parents = lax.slice_in_dim(values, 0, length, 2 * spacing, dimension)
    beside = jnp.roll(parents, -1, dimension)
    selector = [slice(None)] * values.ndim
    selector[dimension] = slice(spacing, length, 2 * spacing)
    return values.at[tuple(selector)].add(orientation * 0.5 * (parents + beside))


def spacings(length, orientation):
    ladder = [2 ** exponent for exponent in range(length.bit_length() - 1)]
    return ladder if orientation < 0 else ladder[::-1]


def sweep(values, dimensions, orientation):
    for dimension in dimensions:
        for spacing in spacings(values.shape[dimension], orientation):
            values = level_pass(values, dimension, spacing, orientation)
    return values


def local_shape(row_count, second_len):
    return (row_count, second_len, 2 ** LOW, 2 ** (LOW + 1), 2 ** (LOW + 2), 2 ** (LOW + 3))


def stencil_numbers(level_row, diffusion, courant):
    matches = (level_row[:, None] == (LOW + jnp.arange(4, dtype=jnp.int32))[None, :]).astype(jnp.float32)
    local_diff = jnp.sum(diffusion[2:, None] * matches, axis=0)
    local_cour = jnp.sum(courant[2:, None] * matches, axis=0)
    return jnp.concatenate([diffusion[:2], local_diff]), jnp.concatenate([courant[:2], local_cour])


def stencil_update(center, forward_rows, backward_rows, diff_num, cour_num):
    update = diff_num[0] * (forward_rows + backward_rows - 2.0 * center) - 0.5 * cour_num[0] * (forward_rows - backward_rows)
    for dimension in range(1, 6):
        forward = jnp.roll(center, -1, dimension)
        backward = jnp.roll(center, 1, dimension)
        update = update + diff_num[dimension] * (forward + backward - 2.0 * center) - 0.5 * cour_num[dimension] * (forward - backward)
    return center + update


def subspace_map(level_row):
    side_len = 2 ** LOW
    entries = side_len ** 4
    flat_ids = jnp.arange(entries, dtype=jnp.int32)
    target = jnp.zeros((entries,), jnp.int32)
    for physical in range(4):
        digits = (flat_ids // side_len ** (3 - physical)) % side_len
        stored = (level_row[physical] - LOW).astype(jnp.int32)
        target = target + digits * jnp.power(side_len, 3 - stored).astype(jnp.int32)
    return (flat_ids[:, None] == target[None, :]).astype(jnp.float32)


def reference(state_field, level_vectors, combine_weights, diffusion, courant):
    nodes = state_field.shape[1]
    side_len = 2 ** LOW
    hierarchized = []
    projected = []
    for member in range(GRIDS):
        diff_num, cour_num = stencil_numbers(level_vectors[member], diffusion, courant)
        values = state_field[member].reshape(local_shape(nodes, SECOND))
        for repeat in range(2):
            values = stencil_update(values, jnp.roll(values, -1, 0), jnp.roll(values, 1, 0), diff_num, cour_num)
        values = sweep(values, [2, 3, 4, 5], -1.0)
        mapping = subspace_map(level_vectors[member])
        shared = values[:, :, :, ::2, ::4, ::8].reshape(nodes * SECOND, side_len ** 4)
        weighted = combine_weights[member].astype(jnp.float32) * jnp.dot(shared, mapping, precision=lax.Precision.HIGHEST)
        projected.append(weighted)
        hierarchized.append(values)
    combined = projected[0]
    for weighted in projected[1:]:
        combined = combined + weighted
    results = []
    for member in range(GRIDS):
        mapping = subspace_map(level_vectors[member])
        returned = jnp.dot(combined, mapping.T, precision=lax.Precision.HIGHEST)
        values = hierarchized[member].at[:, :, :, ::2, ::4, ::8].set(returned.reshape(nodes, SECOND, side_len, side_len, side_len, side_len))
        values = sweep(values, [2, 3, 4, 5], 1.0)
        results.append(values.reshape(nodes, SECOND, -1))
    return jnp.stack(results)
```

```python
import jax
import jax.numpy as jnp
from jax import lax
from jax.experimental import pallas as pl
from jax.experimental.pallas import tpu as pltpu
from jax.sharding import PartitionSpec as P

AXES = ("grid", "dom")
VMEM = pltpu.VMEM
SMEM = pltpu.SMEM
F32 = jnp.float32
BF16 = jnp.bfloat16
LANES = 128
COLS = 16384


def roll(x, shift, axis):
    return pltpu.roll(x, shift, axis)


def numbers(level_ref, diff_ref, cour_ref):
    kappa = [diff_ref[0], diff_ref[1]]
    sigma = [cour_ref[0], cour_ref[1]]
    for j in range(4):
        k, s = F32(0.0), F32(0.0)
        for p in range(4):
            hit = level_ref[0, p] == 2 + j
            k = jnp.where(hit, diff_ref[2 + p], k)
            s = jnp.where(hit, cour_ref[2 + p], s)
        kappa.append(k)
        sigma.append(s)
    fwd = [k - 0.5 * s for k, s in zip(kappa, sigma)]
    bwd = [k + 0.5 * s for k, s in zip(kappa, sigma)]
    centre = 1.0 - 2.0 * (kappa[0] + kappa[1] + kappa[2] + kappa[3] + kappa[4] + kappa[5])
    return fwd, bwd, centre


def parity():
    return lax.axis_index("dom") % 2


def sides(fwd, bwd, p):
    off = jnp.where(p == 0, bwd[0], fwd[0])
    core = jnp.where(p == 0, fwd[0], bwd[0])
    return off, core


def at(i2, d3, c4):
    start = (i2 * 32 + d3 * 4 + c4) * LANES
    return pl.ds(pl.multiple_of(start, LANES), LANES)


def stencil(load, emit, i2, nums):
    fwd, bwd, centre = nums
    lane = lax.broadcasted_iota(jnp.int32, (8, LANES), 1)
    inner = lane % 32
    not_top, not_low = lane < 96, lane >= 32
    not_last, not_first = inner < 31, inner > 0
    above, below = (i2 + 1) % 4, (i2 + 3) % 4
    for d3 in range(8):
        v = [load(i2, d3, c) for c in range(4)]
        ahead = [roll(x, 96, 1) for x in v]
        behind = [roll(x, 32, 1) for x in v]
        for c in range(4):
            x = v[c]
            total = centre * x
            total += fwd[1] * roll(x, 7, 0) + bwd[1] * roll(x, 1, 0)
            total += fwd[2] * load(above, d3, c) + bwd[2] * load(below, d3, c)
            total += fwd[3] * load(i2, (d3 + 1) % 8, c) + bwd[3] * load(i2, (d3 + 7) % 8, c)
            total += fwd[4] * jnp.where(not_top, ahead[c], ahead[(c + 1) % 4])
            total += bwd[4] * jnp.where(not_low, behind[c], behind[(c + 3) % 4])
            total += fwd[5] * jnp.where(not_last, roll(x, 127, 1), roll(x, 31, 1))
            total += bwd[5] * jnp.where(not_first, roll(x, 1, 1), roll(x, 97, 1))
            emit(i2, d3, c, total)


def spots():
    for v in range(2):
        for g in range(4):
            for j in range(8):
                i2 = v * 2 + g // 2
                i3 = (g % 2) * 2 + j // 4
                yield v, g, j, i2, i3, j % 4


def pack(load):
    lane = lax.broadcasted_iota(jnp.int32, (8, LANES), 1)
    code = lane // 32 * 8 + lane % 8
    out = [None, None]
    for v, g, j, i2, i3, i4 in spots():
        x = load(i2, 2 * i3, i4)
        shift = 32 * g + j
        x = roll(x, shift, 1) if shift else x
        out[v] = x if out[v] is None else jnp.where(code == 8 * g + j, x, out[v])
    return jnp.concatenate(out, axis=1)


def first_kernel(u_ref, level_ref, diff_ref, cour_ref, z_ref, near_ref, far_ref):
    nums = numbers(level_ref, diff_ref, cour_ref)
    fwd, bwd, _ = nums
    p = parity()

    def body(step, carry):
        r, i2 = step // 4, step % 4
        other = 1 - r
        factor = 2.0 * jnp.where(r == 0, fwd[0], bwd[0])

        def load(a, b, c):
            return u_ref[r, :, at(a, b, c)]

        def emit(a, b, c, value):
            s = at(a, b, c)
            z_ref[r, :, s] = value + factor * u_ref[other, :, s]

        stencil(load, emit, i2, nums)
        return carry

    lax.fori_loop(0, 8, body, 0)

    def copy(i, carry):
        s = pl.ds(pl.multiple_of(i * 2048, 2048), 2048)
        near_ref[:, s] = u_ref[p, :, s]
        far_ref[:, s] = u_ref[1 - p, :, s]
        return carry

    lax.fori_loop(0, 8, copy, 0)


def storage_index(packed):
    i2 = packed // 64
    i3 = packed // 32 % 2 * 2 + packed // 4 % 2
    i5 = packed // 8 % 4
    return i2 * 64 + i3 * 16 + packed % 4 * 4 + i5


def point_table(level_ref):
    rows = storage_index(lax.broadcasted_iota(jnp.int32, (256, LANES), 0))
    physical = jnp.zeros((256, LANES), jnp.int32)
    for p in range(4):
        stored = level_ref[0, p] - 2
        physical = physical | (((rows >> (2 * (3 - stored))) & 3) << (2 * (3 - p)))
    halves = []
    for half in range(2):
        cols = storage_index(lax.broadcasted_iota(jnp.int32, (8, LANES), 1) + half * LANES)
        halves.append(jnp.where(physical == cols[0:1], 1.0, 0.0))
    return jnp.concatenate(halves, axis=1).astype(BF16)


def exact_dot(x, table, across):
    high = x.astype(BF16)
    rest = x - high.astype(F32)
    middle = rest.astype(BF16)
    low = (rest - middle.astype(F32)).astype(BF16)
    dims = (((1,), (1 if across else 0,)), ((), ()))
    parts = jnp.concatenate([high, middle, low], axis=0)
    done = lax.dot_general(parts, table, dims, preferred_element_type=F32)
    n = x.shape[0]
    return done[:n] + (done[n : 2 * n] + done[2 * n :])


def second_kernel(
    u_ref,
    z_ref,
    k_ref,
    level_ref,
    diff_ref,
    cour_ref,
    weight_ref,
    acc_ref,
    t_ref,
    own_ref,
    off_ref,
    map_ref,
    full_ref,
):
    nums = numbers(level_ref, diff_ref, cour_ref)
    fwd, bwd, _ = nums
    p = parity()
    q = 1 - p
    _, s_core = sides(fwd, bwd, p)
    twice = 2.0 * fwd[0] * bwd[0]
    square, double = s_core * s_core, 2.0 * s_core
    x = pack(lambda a, b, c: u_ref[p, :, at(a, b, c)])
    y = pack(lambda a, b, c: u_ref[q, :, at(a, b, c)])
    zx = pack(lambda a, b, c: z_ref[p, :, at(a, b, c)])
    off_ref[0:8, :] = double * zx - 3.0 * square * y
    off_ref[8:16, :] = square * x

    def add(i, carry):
        s = pl.ds(pl.multiple_of(i * 2048, 2048), 2048)
        full_ref[q, :, s] = z_ref[q, :, s] + double * k_ref[p, :, s]
        return carry

    lax.fori_loop(0, 8, add, 0)

    def body(step, carry):
        r, i2 = step // 4, step % 4

        def load(a, b, c):
            return full_ref[r, :, at(a, b, c)]

        def emit(a, b, c, value):
            s = at(a, b, c)
            acc_ref[r, :, s] = value + twice * u_ref[r, :, s] + square * k_ref[r, :, s]

        stencil(load, emit, i2, nums)
        return carry

    lax.fori_loop(0, 8, body, 0)
    own_ref[0:8, :] = pack(lambda a, b, c: acc_ref[p, :, at(a, b, c)])
    own_ref[8:16, :] = pack(lambda a, b, c: acc_ref[q, :, at(a, b, c)])
    table = point_table(level_ref)
    map_ref[...] = table
    weight = weight_ref[0].astype(F32)
    both = jnp.concatenate([own_ref[...], off_ref[...]], axis=0)
    t_ref[...] = weight * exact_dot(both, table, False)


def gather_kernel(t_ref, a_ref, b_ref, c_ref, off_ref, far_ref, cross_ref, own_ref):
    total = (t_ref[...] + a_ref[...]) + (b_ref[...] + c_ref[...])
    own_ref[...] = total[0:16]
    cross_ref[...] = total[16:32]
    far_ref[0:16, :] = total[16:32]
    far_ref[16:32, :] = off_ref[...]


def near_kernel(acc_ref, zones_ref, same_ref, level_ref, diff_ref, cour_ref, out_ref, near_ref):
    nums = numbers(level_ref, diff_ref, cour_ref)
    fwd, bwd, _ = nums
    p = parity()
    q = 1 - p
    s_off, _ = sides(fwd, bwd, p)
    square, double = s_off * s_off, 2.0 * s_off

    def gather(i, carry):
        s = pl.ds(pl.multiple_of(i * 2048, 2048), 2048)
        near_ref[:, s] = zones_ref[q, :, s] + same_ref[:, s]
        return carry

    lax.fori_loop(0, 8, gather, 0)

    def body(i2, carry):
        def load(a, b, c):
            return near_ref[:, at(a, b, c)]

        def emit(a, b, c, value):
            s = at(a, b, c)
            out_ref[p, :, s] = acc_ref[p, :, s] + double * value
            out_ref[q, :, s] = acc_ref[q, :, s] + square * near_ref[:, s]

        stencil(load, emit, i2, nums)
        return carry

    lax.fori_loop(0, 4, body, 0)


def change_kernel(acc_ref, own_ref, sum_ref, far_ref, cross_ref, flip_ref, map_ref, out_ref, chunks_ref, wide_ref):
    p = parity()
    total = (sum_ref[...] + flip_ref[...]) + (far_ref[0:16, :] + cross_ref[...])
    own = own_ref[...] + far_ref[16:32, :]
    change = exact_dot(total, map_ref[...], True) - own
    for v, g, j, i2, i3, i4 in spots():
        k = (i2 * 4 + i3) * 4 + i4
        x = change[:, v * LANES : (v + 1) * LANES]
        shift = 32 * g + j
        chunks_ref[k * 16 : (k + 1) * 16, :] = roll(x, LANES - shift, 1) if shift else x
    source = lax.broadcasted_iota(jnp.int32, (LANES, 256), 0)
    target = lax.broadcasted_iota(jnp.int32, (LANES, 256), 1)
    lane = target % LANES
    step = lane // 32
    near = jnp.where(target < LANES, 4 - step, step)
    gap = (lane % 32 - source + 32) % 32
    reach = 8 - jnp.minimum(gap, 32 - gap)
    point = (source % 8 == 0) & (source < 32) & (reach > 0)
    table = jnp.where(point, (near * reach).astype(F32) * (1.0 / 32.0), 0.0).astype(BF16)
    wide_ref[...] = exact_dot(chunks_ref[...], table, False)
    rows = ((0, p), (1, 1 - p))

    def plane(i2, i3, c):
        here = wide_ref[pl.ds(pl.multiple_of((i2 * 16 + i3 * 4 + c) * 16, 16), 16), 0:LANES]
        there = wide_ref[pl.ds(pl.multiple_of((i2 * 16 + i3 * 4 + (c + 1) % 4) * 16, 16), 16), LANES:256]
        return here + there

    def body(i2, carry):
        for c in range(4):
            planes = [plane(i2, i3, c) for i3 in range(4)]
            for d3 in range(8):
                value = planes[d3 // 2]
                if d3 % 2:
                    value = 0.5 * (value + planes[(d3 // 2 + 1) % 4])
                s = at(i2, d3, c)
                for half, r in rows:
                    out_ref[r, :, s] = acc_ref[r, :, s] + value[half * 8 : half * 8 + 8]
        return carry

    lax.fori_loop(0, 4, body, 0)


PARTS = 4


def last_kernel(acc_ref, zones_ref, same_ref, diff_ref, cour_ref, out_ref, row_ref, sems):
    p = parity()
    q = 1 - p
    fwd = [diff_ref[0] - 0.5 * cour_ref[0]]
    bwd = [diff_ref[0] + 0.5 * cour_ref[0]]
    s_off, _ = sides(fwd, bwd, p)
    square = s_off * s_off
    whole_row = pltpu.make_async_copy(acc_ref.at[q], out_ref.at[q], sems.at[PARTS])
    whole_row.start()
    width = COLS // PARTS
    copies = []
    for i in range(PARTS):
        s = pl.ds(i * width, width)
        row_ref[:, s] = acc_ref[p, :, s] + square * (zones_ref[p, :, s] + same_ref[:, s])
        copy = pltpu.make_async_copy(row_ref.at[:, s], out_ref.at[p, :, s], sems.at[i])
        copy.start()
        copies.append(copy)
    whole_row.wait()
    for copy in copies:
        copy.wait()


def call(kernel, outs, spaces, scratch=(), aliases=None, space=VMEM):
    return pl.pallas_call(
        kernel,
        out_shape=[jax.ShapeDtypeStruct(s, d) for s, d in outs],
        in_specs=[pl.BlockSpec(memory_space=m) for m in spaces],
        out_specs=[pl.BlockSpec(memory_space=space) for _ in outs],
        scratch_shapes=list(scratch),
        input_output_aliases=aliases or {},
        compiler_params=pltpu.CompilerParams(vmem_limit_bytes=24 * 2**20),
        cost_estimate=pl.CostEstimate(flops=1000, bytes_accessed=1000, transcendentals=0),
    )


def whole(state_field, level_vectors, combine_weights, diffusion, courant):
    u = state_field[0]
    shape = u.shape
    grids, doms = lax.axis_size("grid"), lax.axis_size("dom")
    pairs_same, pairs_zone = [], []
    for d in range(doms):
        right = (d + 1) % doms
        if d % 2:
            (pairs_same if d % 4 == 1 else pairs_zone).extend([(d, right), (right, d)])
    pairs_off = pairs_same + pairs_zone
    pairs_core = [(d, d ^ 1) for d in range(doms)]
    half = grids // 2
    pairs_flip = [(g, (g + half) % grids) for g in range(grids)]
    pairs_cross = [(g * doms + s, (g + half) % grids * doms + t) for g in range(grids) for s, t in pairs_off]

    numbers_in = (level_vectors, diffusion, courant)
    row, points = (shape[1], shape[2]), (16, 256)
    cores = lax.ppermute(u, "dom", pairs_core)
    zones = lax.ppermute(u, "dom", pairs_zone)
    z, near, far_row = call(first_kernel, [(shape, F32), (row, F32), (row, F32)], [VMEM] + [SMEM] * 3)(u, *numbers_in)
    same_near = lax.ppermute(near, "dom", pairs_same)
    acc, t, own, off, table, _ = call(
        second_kernel,
        [(shape, F32), ((32, 256), F32), (points, F32), (points, F32), ((256, 256), BF16), (shape, F32)],
        [VMEM] * 3 + [SMEM] * 4,
        aliases={1: 5},
    )(u, z, cores, *numbers_in, combine_weights)
    turned = []
    for k in range(1, half):
        pairs = [(g, g // half * half + (g + k) % half) for g in range(grids)]
        turned.append(lax.ppermute(t, "grid", pairs))
    far, cross, total = call(gather_kernel, [((32, 256), F32), (points, F32), (points, F32)], [VMEM] * 5)(
        t, *turned, off
    )
    far_in = lax.ppermute(far, "dom", pairs_off)
    cross_in = lax.ppermute(cross, AXES, pairs_cross)
    flip_in = lax.ppermute(total, "grid", pairs_flip)
    same_far = lax.ppermute(far_row, "dom", pairs_same)
    (acc,) = call(
        near_kernel,
        [(shape, F32)],
        [VMEM] * 3 + [SMEM] * 3,
        scratch=[VMEM(row, F32)],
        aliases={0: 0},
    )(acc, zones, same_near, *numbers_in)
    (acc,) = call(
        change_kernel,
        [(shape, F32)],
        [VMEM] * 7,
        scratch=[VMEM((1024, LANES), F32), VMEM((1024, 256), F32)],
        aliases={0: 0},
    )(acc, own, total, far_in, cross_in, flip_in, table)
    (out,) = call(
        last_kernel,
        [(shape, F32)],
        [VMEM] * 3 + [SMEM] * 2,
        scratch=[VMEM(row, F32), pltpu.SemaphoreType.DMA((PARTS + 1,))],
        space=pl.ANY,
    )(acc, zones, same_far, diffusion, courant)
    return out[None]


def solution(mesh):
    placed = (P("grid", "dom", None, None), P("grid", None), P("grid"), P(), P())
    return jax.shard_map(whole, mesh=mesh, in_specs=placed, out_specs=P("grid", "dom", None, None), check_vma=False)
```

```python
import jax
import jax.numpy as jnp
from jax import lax
from jax.experimental import pallas as pl
from jax.experimental.pallas import tpu as pltpu
from jax.sharding import PartitionSpec as P

VMEM = pltpu.VMEM
SMEM = pltpu.SMEM
F32 = jnp.float32
BF16 = jnp.bfloat16
LANES = 128
COLS = 16384
MORE = 8192


def roll(x, shift, axis):
    return pltpu.roll(x, shift, axis)


def numbers(level_ref, diff_ref, cour_ref):
    kappa = [diff_ref[0], diff_ref[1]]
    sigma = [cour_ref[0], cour_ref[1]]
    for j in range(4):
        k, s = F32(0.0), F32(0.0)
        for p in range(4):
            hit = level_ref[0, p] == 2 + j
            k = jnp.where(hit, diff_ref[2 + p], k)
            s = jnp.where(hit, cour_ref[2 + p], s)
        kappa.append(k)
        sigma.append(s)
    fwd = [k - 0.5 * s for k, s in zip(kappa, sigma)]
    bwd = [k + 0.5 * s for k, s in zip(kappa, sigma)]
    centre = 1.0 - 2.0 * (kappa[0] + kappa[1] + kappa[2] + kappa[3] + kappa[4] + kappa[5])
    return fwd, bwd, centre


def parity():
    return lax.axis_index("dom") % 2


def across_layers():
    d = lax.axis_index("dom") % 4
    return (d == 0) | (d == 3)


def sides(fwd, bwd, p):
    off = jnp.where(p == 0, bwd[0], fwd[0])
    core = jnp.where(p == 0, fwd[0], bwd[0])
    return off, core


BAND = 4096


def band(ref, i2):
    start = pl.multiple_of(i2 * BAND, BAND)
    return ref.at[:, pl.ds(start, BAND)]


def chunk(d3, c4):
    start = (d3 * 4 + c4) * LANES
    return slice(start, start + LANES)


def stencil(source, prepare, finish, i2, nums):
    fwd, bwd, centre = nums
    lane = lanes()
    inner = lane % 32
    not_top, not_low = lane < 96, lane >= 32
    first, last = inner == 0, inner == 31
    here, above, below = band(source, i2), band(source, (i2 + 1) % 4), band(source, (i2 + 3) % 4)
    group = lambda ref, d3: [ref[:, chunk(d3 % 8, c)] for c in range(4)]
    low, v = group(here, 7), group(here, 0)
    waiting = None
    for d3 in range(8):
        high, over, under = group(here, d3 + 1), group(above, d3), group(below, d3)
        beside = [prepare(chunk(d3, c)) for c in range(4)]
        ahead = [roll(x, 96, 1) for x in v]
        behind = [roll(x, 32, 1) for x in v]
        done = []
        for c in range(4):
            x = v[c]
            total = centre * x
            total += fwd[1] * roll(x, 7, 0) + bwd[1] * roll(x, 1, 0)
            total += fwd[2] * over[c] + bwd[2] * under[c]
            total += fwd[3] * high[c] + bwd[3] * low[c]
            total += fwd[4] * jnp.where(not_top, ahead[c], ahead[(c + 1) % 4])
            total += bwd[4] * jnp.where(not_low, behind[c], behind[(c + 3) % 4])
            total += fwd[5] * roll(jnp.where(first, behind[c], x), 127, 1)
            total += bwd[5] * roll(jnp.where(last, ahead[c], x), 1, 1)
            done.append(total)
        if waiting is not None:
            for item in waiting:
                finish(*item)
        waiting = [(chunk(d3, c), done[c], beside[c]) for c in range(4)]
        low, v = v, high
    for item in waiting:
        finish(*item)


def stream(i2, out, rule, *sources):
    out = band(out, i2)
    sources = [band(x, i2) for x in sources]
    for i in range(0, 32, 8):
        places = [slice((i + j) * LANES, (i + j + 1) * LANES) for j in range(8)]
        values = [rule(*[x[:, s] for x in sources]) for s in places]
        for s, value in zip(places, values):
            out[:, s] = value


def lanes():
    return lax.broadcasted_iota(jnp.int32, (8, LANES), 1)


def spots():
    for v in range(2):
        for i4 in range(4):
            for j in range(8):
                yield v, j, 2 * v + j % 2, j // 2, i4


def pack(load):
    code = lanes() // 32 * 8 + lanes() % 8
    out = [None, None]
    for v, j, i2, i3, i4 in spots():
        start = i2 * BAND + (i3 * 8 + i4) * LANES
        x = load(slice(start, start + LANES))
        shift = 32 * i4 + j
        x = roll(x, shift, 1) if shift else x
        out[v] = x if out[v] is None else jnp.where(code == 8 * i4 + j, x, out[v])
    return jnp.concatenate(out, axis=1)


def first_kernel(
    u_ref, level_ref, diff_ref, cour_ref, weight_ref, head_ref, tail_ref, z_ref, off_ref, scale_ref, sems
):
    p = parity()
    x_ref, y_ref = u_ref.at[p], u_ref.at[1 - p]
    moves = [
        (u_ref.at[p], head_ref.at[:, pl.ds(0, COLS)]),
        (u_ref.at[1 - p, :, pl.ds(0, MORE)], head_ref.at[:, pl.ds(COLS, MORE)]),
        (u_ref.at[1 - p, :, pl.ds(MORE, COLS - MORE)], tail_ref),
    ]
    copies = [pltpu.make_async_copy(source, target, sems.at[i]) for i, (source, target) in enumerate(moves)]
    for copy in copies:
        copy.start()
    nums = numbers(level_ref, diff_ref, cour_ref)
    fwd, bwd, _ = nums
    s_off, s_core = sides(fwd, bwd, p)
    for r, (own, other, factor) in enumerate(((x_ref, y_ref, 2.0 * s_core), (y_ref, x_ref, 2.0 * s_off))):

        def body(i2, carry):
            beside, out = band(other, i2), band(z_ref.at[r], i2)

            def finish(s, value, extra):
                out[:, s] = value + factor * extra

            stencil(own, lambda s: beside[:, s], finish, i2, nums)
            return carry

        lax.fori_loop(0, 4, body, 0)
    square, double = s_core * s_core, 2.0 * s_core
    off_ref[0:8, :] = pack(lambda s: double * z_ref[0, :, s] - (3.0 * square) * y_ref[:, s])
    off_ref[8:16, :] = square * pack(lambda s: x_ref[:, s])
    scale_ref[...] = jnp.full(scale_ref.shape, weight_ref[0].astype(F32))
    for copy in copies:
        copy.wait()


def storage_index(packed):
    i2 = (packed >> 7) * 2 + (packed & 1)
    return i2 * 64 + ((packed >> 1) & 3) * 16 + ((packed >> 5) & 3) * 4 + ((packed >> 3) & 3)


def point_table(level_ref):
    rows = storage_index(lax.broadcasted_iota(jnp.int32, (256, LANES), 0))
    physical = jnp.zeros((256, LANES), jnp.int32)
    for p in range(4):
        stored = level_ref[0, p] - 2
        physical = physical | (((rows >> (2 * (3 - stored))) & 3) << (2 * (3 - p)))
    halves = []
    for half in range(2):
        cols = storage_index(lax.broadcasted_iota(jnp.int32, (8, LANES), 1) + half * LANES)
        halves.append(jnp.where(physical == cols[0:1], 1.0, 0.0))
    return jnp.concatenate(halves, axis=1).astype(BF16)


def exact_dot(x, table, across):
    high = x.astype(BF16)
    rest = x - high.astype(F32)
    middle = rest.astype(BF16)
    low = (rest - middle.astype(F32)).astype(BF16)
    dims = (((1,), (1 if across else 0,)), ((), ()))
    parts = jnp.concatenate([high, middle, low], axis=0)
    done = lax.dot_general(parts, table, dims, preferred_element_type=F32)
    n = x.shape[0]
    return done[:n] + (done[n : 2 * n] + done[2 * n :])


def second_kernel(
    u_ref,
    z_ref,
    k_ref,
    off_ref,
    level_ref,
    diff_ref,
    cour_ref,
    scale_ref,
    acc_ref,
    full_ref,
    own_ref,
    t_ref,
    map_ref,
):
    nums = numbers(level_ref, diff_ref, cour_ref)
    fwd, bwd, _ = nums
    p = parity()
    q = 1 - p
    _, s_core = sides(fwd, bwd, p)
    twice = 2.0 * fwd[0] * bwd[0]
    square, double = s_core * s_core, 2.0 * s_core

    def add(i2, carry):
        stream(i2, full_ref.at[1], lambda a, b: a + double * b, z_ref.at[1], k_ref.at[p])
        return carry

    lax.fori_loop(0, 4, add, 0)
    for r, (own, core) in enumerate(((u_ref.at[p], p), (u_ref.at[q], q))):

        def body(i2, carry):
            here, there, out = band(own, i2), band(k_ref.at[core], i2), band(acc_ref.at[r], i2)

            def finish(s, value, extra):
                out[:, s] = value + extra

            stencil(full_ref.at[r], lambda s: twice * here[:, s] + square * there[:, s], finish, i2, nums)
            return carry

        lax.fori_loop(0, 4, body, 0)
    own_ref[0:8, :] = pack(lambda s: acc_ref[0, :, s])
    own_ref[8:16, :] = pack(lambda s: acc_ref[1, :, s])
    table = point_table(level_ref)
    map_ref[...] = table
    weight = scale_ref[0:1, 0:1]
    both = jnp.concatenate([own_ref[...], off_ref[...]], axis=0)
    t_ref[...] = weight * exact_dot(both, table, False)


def gather_kernel(t_ref, a_ref, b_ref, c_ref, off_ref, far_ref, cross_ref, own_ref):
    total = (t_ref[...] + a_ref[...]) + (b_ref[...] + c_ref[...])
    own_ref[...] = total[0:16]
    cross_ref[...] = total[16:32]
    far_ref[0:16, :] = total[16:32]
    far_ref[16:32, :] = off_ref[...]


def near_kernel(acc_ref, zones_ref, same_ref, level_ref, diff_ref, cour_ref, out_ref, near_ref):
    nums = numbers(level_ref, diff_ref, cour_ref)
    fwd, bwd, _ = nums
    p = parity()
    layers = across_layers()
    s_off, _ = sides(fwd, bwd, p)
    square, double = s_off * s_off, 2.0 * s_off

    def gather(i2, carry):
        stream(i2, near_ref, lambda a, b: jnp.where(layers, a, b), zones_ref.at[1 - p], same_ref)
        return carry

    lax.fori_loop(0, 4, gather, 0)

    def body(i2, carry):
        near = band(near_ref, i2)
        old = [band(acc_ref.at[r], i2) for r in range(2)]
        new = [band(out_ref.at[r], i2) for r in range(2)]

        def prepare(s):
            return old[0][:, s], old[1][:, s] + square * near[:, s]

        def finish(s, value, extra):
            new[0][:, s] = extra[0] + double * value
            new[1][:, s] = extra[1]

        stencil(near_ref, prepare, finish, i2, nums)
        return carry

    lax.fori_loop(0, 4, body, 0)


def far_square(diff_ref, cour_ref, p):
    fwd = [diff_ref[0] - 0.5 * cour_ref[0]]
    bwd = [diff_ref[0] + 0.5 * cour_ref[0]]
    s_off, _ = sides(fwd, bwd, p)
    return s_off * s_off


def change_kernel(
    acc_ref,
    own_ref,
    sum_ref,
    far_ref,
    cross_ref,
    flip_ref,
    map_ref,
    zones_ref,
    head_ref,
    diff_ref,
    cour_ref,
    out_ref,
    rest_ref,
    chunks_ref,
    wide_ref,
    x_ref,
    y_ref,
    sems,
):
    p = parity()
    square = far_square(diff_ref, cour_ref, p)
    layers = across_layers()
    late_square = jnp.where(layers, square, 0.0)
    total = (sum_ref[...] + flip_ref[...]) + (far_ref[0:16, :] + cross_ref[...])
    own = own_ref[...] + far_ref[16:32, :]
    change = exact_dot(total, map_ref[...], True) - own
    for v, j, i2, i3, i4 in spots():
        k = (i2 * 4 + i3) * 4 + i4
        x = change[:, v * LANES : (v + 1) * LANES]
        shift = 32 * i4 + j
        chunks_ref[k * 16 : (k + 1) * 16, :] = roll(x, LANES - shift, 1) if shift else x
    source = lax.broadcasted_iota(jnp.int32, (LANES, 256), 0)
    target = lax.broadcasted_iota(jnp.int32, (LANES, 256), 1)
    lane = target % LANES
    step = lane // 32
    near = jnp.where(target < LANES, 4 - step, step)
    gap = (lane % 32 - source + 32) % 32
    reach = 8 - jnp.minimum(gap, 32 - gap)
    point = (source % 8 == 0) & (source < 32) & (reach > 0)
    table = jnp.where(point, (near * reach).astype(F32) * (1.0 / 32.0), 0.0).astype(BF16)
    wide_ref[...] = exact_dot(chunks_ref[...], table, False)
    copies = []
    for i2 in range(4):
        for c in range(4):
            planes = []
            for i3 in range(4):
                k, m = (i2 * 16 + i3 * 4 + c) * 16, (i2 * 16 + i3 * 4 + (c + 1) % 4) * 16
                planes.append(wide_ref[k : k + 16, 0:LANES] + wide_ref[m : m + 16, LANES:256])
            for d3 in range(8):
                value = planes[d3 // 2]
                if d3 % 2:
                    value = 0.5 * (value + planes[(d3 // 2 + 1) % 4])
                start = i2 * BAND + (d3 * 4 + c) * LANES
                s = slice(start, start + LANES)
                ready = acc_ref[0, :, s] + value[0:8]
                if start < MORE:
                    far = jnp.where(layers, zones_ref[p, :, s], head_ref[:, COLS + start : COLS + start + LANES])
                    x_ref[:, s] = ready + square * far
                else:
                    rest_ref[:, start - MORE : start - MORE + LANES] = ready + late_square * zones_ref[p, :, s]
                y_ref[:, s] = acc_ref[1, :, s] + value[8:16]
        s = pl.ds(i2 * BAND, BAND)
        copies.append(pltpu.make_async_copy(y_ref.at[:, s], out_ref.at[1 - p, :, s], sems.at[len(copies)]))
        copies[-1].start()
        if i2 * BAND < MORE:
            copies.append(pltpu.make_async_copy(x_ref.at[:, s], out_ref.at[p, :, s], sems.at[len(copies)]))
            copies[-1].start()
    late = pltpu.make_async_copy(rest_ref, out_ref.at[p, :, pl.ds(MORE, COLS - MORE)], sems.at[7])

    @pl.when(layers)
    def _():
        late.start()
        late.wait()

    for copy in copies:
        copy.wait()


PARTS = 2


def last_kernel(rest_ref, tail_ref, diff_ref, cour_ref, old_ref, out_ref, row_ref, sems):
    p = parity()
    square = far_square(diff_ref, cour_ref, p)
    width = (COLS - MORE) // PARTS

    @pl.when(jnp.logical_not(across_layers()))
    def _():
        copies = []
        for i in range(PARTS):
            s = slice(i * width, (i + 1) * width)
            row_ref[:, s] = rest_ref[:, s] + square * tail_ref[:, s]
            copy = pltpu.make_async_copy(
                row_ref.at[:, s], out_ref.at[p, :, pl.ds(MORE + s.start, width)], sems.at[i]
            )
            copy.start()
            copies.append(copy)
        for copy in copies:
            copy.wait()


def call(kernel, outs, spaces, scratch=(), aliases=None, space=VMEM):
    return pl.pallas_call(
        kernel,
        out_shape=[jax.ShapeDtypeStruct(s, d) for s, d in outs],
        in_specs=[pl.BlockSpec(memory_space=m) for m in spaces],
        out_specs=[pl.BlockSpec(memory_space=space if i == 0 else VMEM) for i in range(len(outs))],
        scratch_shapes=list(scratch),
        input_output_aliases=aliases or {},
        compiler_params=pltpu.CompilerParams(vmem_limit_bytes=24 * 2**20),
        cost_estimate=pl.CostEstimate(flops=1000, bytes_accessed=1000, transcendentals=0),
    )


def whole(state_field, level_vectors, combine_weights, diffusion, courant):
    u = state_field[0]
    shape = u.shape
    grids, doms = lax.axis_size("grid"), lax.axis_size("dom")
    pairs_same, pairs_zone = [], []
    for d in range(doms):
        right = (d + 1) % doms
        if d % 2:
            (pairs_same if d % 4 == 1 else pairs_zone).extend([(d, right), (right, d)])
    pairs_off = pairs_same + pairs_zone
    pairs_core = [(d, d ^ 1) for d in range(doms)]
    half = grids // 2
    pairs_flip = [(g, (g + half) % grids) for g in range(grids)]
    pairs_cross = [(g * doms + s, (g + half) % grids * doms + t) for g in range(grids) for s, t in pairs_off]

    numbers_in = (level_vectors, diffusion, courant)
    row, points, rest = (shape[1], shape[2]), (16, 256), (8, COLS - MORE)
    cores = lax.ppermute(u, "dom", pairs_core)
    zones = lax.ppermute(u, "dom", pairs_zone)
    head, tail, z, off, scale = call(
        first_kernel,
        [((8, COLS + MORE), F32), (rest, F32), (shape, F32), (points, F32), ((8, LANES), F32)],
        [VMEM] + [SMEM] * 4,
        scratch=[pltpu.SemaphoreType.DMA((3,))],
    )(u, *numbers_in, combine_weights)
    same_head = lax.ppermute(head, "dom", pairs_same)
    acc, _, own, t, table = call(
        second_kernel,
        [(shape, F32), (shape, F32), (points, F32), ((32, 256), F32), ((256, 256), BF16)],
        [VMEM] * 4 + [SMEM] * 3 + [VMEM],
        aliases={1: 1},
    )(u, z, cores, off, *numbers_in, scale)
    turned = []
    for k in range(1, half):
        pairs = [(g, g // half * half + (g + k) % half) for g in range(grids)]
        turned.append(lax.ppermute(t, "grid", pairs))
    far, cross, total = call(gather_kernel, [((32, 256), F32), (points, F32), (points, F32)], [VMEM] * 5)(
        t, *turned, off
    )
    far_in = lax.ppermute(far, "dom", pairs_off)
    cross_in = lax.ppermute(cross, ("grid", "dom"), pairs_cross)
    flip_in = lax.ppermute(total, "grid", pairs_flip)
    same_tail = lax.ppermute(tail, "dom", pairs_same)
    (acc,) = call(
        near_kernel,
        [(shape, F32)],
        [VMEM] * 3 + [SMEM] * 3,
        scratch=[VMEM(row, F32)],
        aliases={0: 0},
    )(acc, zones, same_head, *numbers_in)
    out, kept = call(
        change_kernel,
        [(shape, F32), (rest, F32)],
        [VMEM] * 9 + [SMEM] * 2,
        scratch=[
            VMEM((1024, LANES), F32),
            VMEM((1024, 256), F32),
            VMEM((8, MORE), F32),
            VMEM(row, F32),
            pltpu.SemaphoreType.DMA((8,)),
        ],
        space=pltpu.HBM,
    )(acc, own, total, far_in, cross_in, flip_in, table, zones, same_head, diffusion, courant)
    (out,) = call(
        last_kernel,
        [(shape, F32)],
        [VMEM] * 2 + [SMEM] * 2 + [pltpu.HBM],
        scratch=[VMEM(rest, F32), pltpu.SemaphoreType.DMA((PARTS,))],
        aliases={4: 0},
        space=pltpu.HBM,
    )(kept, same_tail, diffusion, courant, out)
    return out[None]


def solution(mesh):
    placed = (P("grid", "dom", None, None), P("grid", None), P("grid"), P(), P())
    return jax.shard_map(whole, mesh=mesh, in_specs=placed, out_specs=P("grid", "dom", None, None), check_vma=False)
```

```python
import jax
import jax.numpy as jnp
from jax import lax
from jax.experimental import pallas as pl
from jax.experimental.pallas import tpu as pltpu
from jax.sharding import PartitionSpec as P

VMEM = pltpu.VMEM
SMEM = pltpu.SMEM
F32 = jnp.float32
BF16 = jnp.bfloat16
LANES = 128
COLS = 16384
MORE = 8192


def roll(x, shift, axis):
    return pltpu.roll(x, shift, axis)


def numbers(level_ref, diff_ref, cour_ref):
    kappa = [diff_ref[0], diff_ref[1]]
    sigma = [cour_ref[0], cour_ref[1]]
    for j in range(4):
        k, s = F32(0.0), F32(0.0)
        for p in range(4):
            hit = level_ref[0, p] == 2 + j
            k = jnp.where(hit, diff_ref[2 + p], k)
            s = jnp.where(hit, cour_ref[2 + p], s)
        kappa.append(k)
        sigma.append(s)
    fwd = [k - 0.5 * s for k, s in zip(kappa, sigma)]
    bwd = [k + 0.5 * s for k, s in zip(kappa, sigma)]
    centre = 1.0 - 2.0 * (kappa[0] + kappa[1] + kappa[2] + kappa[3] + kappa[4] + kappa[5])
    return fwd, bwd, centre


def parity():
    return lax.axis_index("dom") % 2


def across_layers():
    d = lax.axis_index("dom") % 4
    return (d == 0) | (d == 3)


def sides(fwd, bwd, p):
    off = jnp.where(p == 0, bwd[0], fwd[0])
    core = jnp.where(p == 0, fwd[0], bwd[0])
    return off, core


BAND = 4096


def band(ref, i2):
    start = pl.multiple_of(i2 * BAND, BAND)
    return ref.at[:, pl.ds(start, BAND)]


def chunk(d3, c4):
    start = (d3 * 4 + c4) * LANES
    return slice(start, start + LANES)


def stencil(source, prepare, finish, i2, nums):
    fwd, bwd, centre = nums
    lane = lanes()
    inner = lane % 32
    not_top, not_low = lane < 96, lane >= 32
    first, last = inner == 0, inner == 31
    here, above, below = band(source, i2), band(source, (i2 + 1) % 4), band(source, (i2 + 3) % 4)
    group = lambda ref, d3: [ref[:, chunk(d3 % 8, c)] for c in range(4)]
    low, v = group(here, 7), group(here, 0)
    waiting = None
    for d3 in range(8):
        high, over, under = group(here, d3 + 1), group(above, d3), group(below, d3)
        beside = [prepare(chunk(d3, c)) for c in range(4)]
        ahead = [roll(x, 96, 1) for x in v]
        behind = [roll(x, 32, 1) for x in v]
        done = []
        for c in range(4):
            x = v[c]
            total = centre * x
            total += fwd[1] * roll(x, 7, 0) + bwd[1] * roll(x, 1, 0)
            total += fwd[2] * over[c] + bwd[2] * under[c]
            total += fwd[3] * high[c] + bwd[3] * low[c]
            total += fwd[4] * jnp.where(not_top, ahead[c], ahead[(c + 1) % 4])
            total += bwd[4] * jnp.where(not_low, behind[c], behind[(c + 3) % 4])
            total += fwd[5] * roll(jnp.where(first, behind[c], x), 127, 1)
            total += bwd[5] * roll(jnp.where(last, ahead[c], x), 1, 1)
            done.append(total)
        if waiting is not None:
            for item in waiting:
                finish(*item)
        waiting = [(chunk(d3, c), done[c], beside[c]) for c in range(4)]
        low, v = v, high
    for item in waiting:
        finish(*item)


def stream(i2, out, rule, *sources):
    out = band(out, i2)
    sources = [band(x, i2) for x in sources]
    for i in range(0, 32, 8):
        places = [slice((i + j) * LANES, (i + j + 1) * LANES) for j in range(8)]
        values = [rule(*[x[:, s] for x in sources]) for s in places]
        for s, value in zip(places, values):
            out[:, s] = value


def lanes():
    return lax.broadcasted_iota(jnp.int32, (8, LANES), 1)


def spots():
    for v in range(2):
        for i4 in range(4):
            for j in range(8):
                yield v, j, 2 * v + j % 2, j // 2, i4


def pack(load):
    code = lanes() // 32 * 8 + lanes() % 8
    out = [None, None]
    for v, j, i2, i3, i4 in spots():
        start = i2 * BAND + (i3 * 8 + i4) * LANES
        x = load(slice(start, start + LANES))
        shift = 32 * i4 + j
        x = roll(x, shift, 1) if shift else x
        out[v] = x if out[v] is None else jnp.where(code == 8 * i4 + j, x, out[v])
    return jnp.concatenate(out, axis=1)


def first_kernel(
    u_ref, level_ref, diff_ref, cour_ref, weight_ref, head_ref, tail_ref, z_ref, off_ref, scale_ref, sems
):
    p = parity()
    x_ref, y_ref = u_ref.at[p], u_ref.at[1 - p]
    moves = [
        (u_ref.at[p], head_ref.at[:, pl.ds(0, COLS)]),
        (u_ref.at[1 - p, :, pl.ds(0, MORE)], head_ref.at[:, pl.ds(COLS, MORE)]),
        (u_ref.at[1 - p, :, pl.ds(MORE, COLS - MORE)], tail_ref),
    ]
    copies = [pltpu.make_async_copy(source, target, sems.at[i]) for i, (source, target) in enumerate(moves)]
    for copy in copies:
        copy.start()
    nums = numbers(level_ref, diff_ref, cour_ref)
    fwd, bwd, _ = nums
    s_off, s_core = sides(fwd, bwd, p)
    for r, (own, other, factor) in enumerate(((x_ref, y_ref, 2.0 * s_core), (y_ref, x_ref, 2.0 * s_off))):

        def body(i2, carry):
            beside, out = band(other, i2), band(z_ref.at[r], i2)

            def finish(s, value, extra):
                out[:, s] = value + factor * extra

            stencil(own, lambda s: beside[:, s], finish, i2, nums)
            return carry

        lax.fori_loop(0, 4, body, 0)
    square, double = s_core * s_core, 2.0 * s_core
    off_ref[0:8, :] = pack(lambda s: double * z_ref[0, :, s] - (3.0 * square) * y_ref[:, s])
    off_ref[8:16, :] = square * pack(lambda s: x_ref[:, s])
    scale_ref[...] = jnp.full(scale_ref.shape, weight_ref[0].astype(F32))
    for copy in copies:
        copy.wait()


def storage_index(packed):
    i2 = (packed >> 7) * 2 + (packed & 1)
    return i2 * 64 + ((packed >> 1) & 3) * 16 + ((packed >> 5) & 3) * 4 + ((packed >> 3) & 3)


def point_table(level_ref):
    rows = storage_index(lax.broadcasted_iota(jnp.int32, (256, LANES), 0))
    physical = jnp.zeros((256, LANES), jnp.int32)
    for p in range(4):
        stored = level_ref[0, p] - 2
        physical = physical | (((rows >> (2 * (3 - stored))) & 3) << (2 * (3 - p)))
    halves = []
    for half in range(2):
        cols = storage_index(lax.broadcasted_iota(jnp.int32, (8, LANES), 1) + half * LANES)
        halves.append(jnp.where(physical == cols[0:1], 1.0, 0.0))
    return jnp.concatenate(halves, axis=1).astype(BF16)


def exact_dot(x, table, across):
    high = x.astype(BF16)
    rest = x - high.astype(F32)
    middle = rest.astype(BF16)
    low = (rest - middle.astype(F32)).astype(BF16)
    dims = (((1,), (1 if across else 0,)), ((), ()))
    parts = jnp.concatenate([high, middle, low], axis=0)
    done = lax.dot_general(parts, table, dims, preferred_element_type=F32)
    n = x.shape[0]
    return done[:n] + (done[n : 2 * n] + done[2 * n :])


def second_kernel(
    u_ref,
    z_ref,
    k_ref,
    off_ref,
    level_ref,
    diff_ref,
    cour_ref,
    scale_ref,
    acc_ref,
    full_ref,
    own_ref,
    t_ref,
    map_ref,
):
    nums = numbers(level_ref, diff_ref, cour_ref)
    fwd, bwd, _ = nums
    p = parity()
    q = 1 - p
    _, s_core = sides(fwd, bwd, p)
    twice = 2.0 * fwd[0] * bwd[0]
    square, double = s_core * s_core, 2.0 * s_core

    def add(i2, carry):
        stream(i2, full_ref.at[1], lambda a, b: a + double * b, z_ref.at[1], k_ref.at[p])
        return carry

    lax.fori_loop(0, 4, add, 0)
    for r, (own, core) in enumerate(((u_ref.at[p], p), (u_ref.at[q], q))):

        def body(i2, carry):
            here, there, out = band(own, i2), band(k_ref.at[core], i2), band(acc_ref.at[r], i2)

            def finish(s, value, extra):
                out[:, s] = value + extra

            stencil(full_ref.at[r], lambda s: twice * here[:, s] + square * there[:, s], finish, i2, nums)
            return carry

        lax.fori_loop(0, 4, body, 0)
    own_ref[0:8, :] = pack(lambda s: acc_ref[0, :, s])
    own_ref[8:16, :] = pack(lambda s: acc_ref[1, :, s])
    table = point_table(level_ref)
    map_ref[...] = table
    weight = scale_ref[0:1, 0:1]
    both = jnp.concatenate([own_ref[...], off_ref[...]], axis=0)
    t_ref[...] = weight * exact_dot(both, table, False)


def gather_kernel(t_ref, a_ref, b_ref, c_ref, off_ref, far_ref, cross_ref, own_ref):
    total = (t_ref[...] + a_ref[...]) + (b_ref[...] + c_ref[...])
    own_ref[...] = total[0:16]
    cross_ref[...] = total[16:32]
    far_ref[0:16, :] = total[16:32]
    far_ref[16:32, :] = off_ref[...]


def near_kernel(acc_ref, zones_ref, same_ref, level_ref, diff_ref, cour_ref, out_ref, near_ref):
    nums = numbers(level_ref, diff_ref, cour_ref)
    fwd, bwd, _ = nums
    p = parity()
    layers = across_layers()
    s_off, _ = sides(fwd, bwd, p)
    square, double = s_off * s_off, 2.0 * s_off

    def gather(i2, carry):
        stream(i2, near_ref, lambda a, b: jnp.where(layers, a, b), zones_ref.at[1 - p], same_ref)
        return carry

    lax.fori_loop(0, 4, gather, 0)

    def body(i2, carry):
        near = band(near_ref, i2)
        old = [band(acc_ref.at[r], i2) for r in range(2)]
        new = [band(out_ref.at[r], i2) for r in range(2)]

        def prepare(s):
            return old[0][:, s], old[1][:, s] + square * near[:, s]

        def finish(s, value, extra):
            new[0][:, s] = extra[0] + double * value
            new[1][:, s] = extra[1]

        stencil(near_ref, prepare, finish, i2, nums)
        return carry

    lax.fori_loop(0, 4, body, 0)


def far_square(diff_ref, cour_ref, p):
    fwd = [diff_ref[0] - 0.5 * cour_ref[0]]
    bwd = [diff_ref[0] + 0.5 * cour_ref[0]]
    s_off, _ = sides(fwd, bwd, p)
    return s_off * s_off


def change_kernel(
    acc_ref,
    own_ref,
    sum_ref,
    far_ref,
    cross_ref,
    flip_ref,
    map_ref,
    zones_ref,
    head_ref,
    diff_ref,
    cour_ref,
    out_ref,
    rest_ref,
    chunks_ref,
    wide_ref,
    x_ref,
    y_ref,
    sems,
):
    p = parity()
    square = far_square(diff_ref, cour_ref, p)
    layers = across_layers()
    late_square = jnp.where(layers, square, 0.0)
    total = (sum_ref[...] + flip_ref[...]) + (far_ref[0:16, :] + cross_ref[...])
    own = own_ref[...] + far_ref[16:32, :]
    change = exact_dot(total, map_ref[...], True) - own
    for v, j, i2, i3, i4 in spots():
        k = (i2 * 4 + i3) * 4 + i4
        x = change[:, v * LANES : (v + 1) * LANES]
        shift = 32 * i4 + j
        chunks_ref[k * 16 : (k + 1) * 16, :] = roll(x, LANES - shift, 1) if shift else x
    source = lax.broadcasted_iota(jnp.int32, (LANES, 256), 0)
    target = lax.broadcasted_iota(jnp.int32, (LANES, 256), 1)
    lane = target % LANES
    step = lane // 32
    near = jnp.where(target < LANES, 4 - step, step)
    gap = (lane % 32 - source + 32) % 32
    reach = 8 - jnp.minimum(gap, 32 - gap)
    point = (source % 8 == 0) & (source < 32) & (reach > 0)
    table = jnp.where(point, (near * reach).astype(F32) * (1.0 / 32.0), 0.0).astype(BF16)
    x = chunks_ref[...]
    high = x.astype(BF16)
    low = (x - high.astype(F32)).astype(BF16)
    dims = (((1,), (0,)), ((), ()))
    parts = lax.dot_general(jnp.concatenate([high, low], axis=0), table, dims, preferred_element_type=F32)
    wide_ref[...] = parts[:1024] + parts[1024:]
    copies = []
    for i2 in range(4):
        for c in range(4):
            planes = []
            for i3 in range(4):
                k, m = (i2 * 16 + i3 * 4 + c) * 16, (i2 * 16 + i3 * 4 + (c + 1) % 4) * 16
                planes.append(wide_ref[k : k + 16, 0:LANES] + wide_ref[m : m + 16, LANES:256])
            for d3 in range(8):
                value = planes[d3 // 2]
                if d3 % 2:
                    value = 0.5 * (value + planes[(d3 // 2 + 1) % 4])
                start = i2 * BAND + (d3 * 4 + c) * LANES
                s = slice(start, start + LANES)
                ready = acc_ref[0, :, s] + value[0:8]
                if start < MORE:
                    far = jnp.where(layers, zones_ref[p, :, s], head_ref[:, COLS + start : COLS + start + LANES])
                    x_ref[:, s] = ready + square * far
                else:
                    rest_ref[:, start - MORE : start - MORE + LANES] = ready + late_square * zones_ref[p, :, s]
                y_ref[:, s] = acc_ref[1, :, s] + value[8:16]
        s = pl.ds(i2 * BAND, BAND)
        copies.append(pltpu.make_async_copy(y_ref.at[:, s], out_ref.at[1 - p, :, s], sems.at[len(copies)]))
        copies[-1].start()
        if i2 * BAND < MORE:
            copies.append(pltpu.make_async_copy(x_ref.at[:, s], out_ref.at[p, :, s], sems.at[len(copies)]))
            copies[-1].start()
    late = pltpu.make_async_copy(rest_ref, out_ref.at[p, :, pl.ds(MORE, COLS - MORE)], sems.at[7])

    @pl.when(layers)
    def _():
        late.start()
        late.wait()

    for copy in copies:
        copy.wait()


PARTS = 2


def last_kernel(rest_ref, tail_ref, diff_ref, cour_ref, old_ref, out_ref, row_ref, sems):
    p = parity()
    square = far_square(diff_ref, cour_ref, p)
    width = (COLS - MORE) // PARTS

    @pl.when(jnp.logical_not(across_layers()))
    def _():
        copies = []
        for i in range(PARTS):
            s = slice(i * width, (i + 1) * width)
            row_ref[:, s] = rest_ref[:, s] + square * tail_ref[:, s]
            copy = pltpu.make_async_copy(
                row_ref.at[:, s], out_ref.at[p, :, pl.ds(MORE + s.start, width)], sems.at[i]
            )
            copy.start()
            copies.append(copy)
        for copy in copies:
            copy.wait()


def call(kernel, outs, spaces, scratch=(), aliases=None, space=VMEM):
    return pl.pallas_call(
        kernel,
        out_shape=[jax.ShapeDtypeStruct(s, d) for s, d in outs],
        in_specs=[pl.BlockSpec(memory_space=m) for m in spaces],
        out_specs=[pl.BlockSpec(memory_space=space if i == 0 else VMEM) for i in range(len(outs))],
        scratch_shapes=list(scratch),
        input_output_aliases=aliases or {},
        compiler_params=pltpu.CompilerParams(vmem_limit_bytes=24 * 2**20),
        cost_estimate=pl.CostEstimate(flops=1000, bytes_accessed=1000, transcendentals=0),
    )


def whole(state_field, level_vectors, combine_weights, diffusion, courant):
    u = state_field[0]
    shape = u.shape
    grids, doms = lax.axis_size("grid"), lax.axis_size("dom")
    pairs_same, pairs_zone = [], []
    for d in range(doms):
        right = (d + 1) % doms
        if d % 2:
            (pairs_same if d % 4 == 1 else pairs_zone).extend([(d, right), (right, d)])
    pairs_off = pairs_same + pairs_zone
    pairs_core = [(d, d ^ 1) for d in range(doms)]
    half = grids // 2
    pairs_flip = [(g, (g + half) % grids) for g in range(grids)]
    pairs_cross = [(g * doms + s, (g + half) % grids * doms + t) for g in range(grids) for s, t in pairs_off]

    numbers_in = (level_vectors, diffusion, courant)
    row, points, rest = (shape[1], shape[2]), (16, 256), (8, COLS - MORE)
    cores = lax.ppermute(u, "dom", pairs_core)
    zones = lax.ppermute(u, "dom", pairs_zone)
    head, tail, z, off, scale = call(
        first_kernel,
        [((8, COLS + MORE), F32), (rest, F32), (shape, F32), (points, F32), ((8, LANES), F32)],
        [VMEM] + [SMEM] * 4,
        scratch=[pltpu.SemaphoreType.DMA((3,))],
    )(u, *numbers_in, combine_weights)
    same_head = lax.ppermute(head, "dom", pairs_same)
    acc, _, own, t, table = call(
        second_kernel,
        [(shape, F32), (shape, F32), (points, F32), ((32, 256), F32), ((256, 256), BF16)],
        [VMEM] * 4 + [SMEM] * 3 + [VMEM],
        aliases={1: 1},
    )(u, z, cores, off, *numbers_in, scale)
    turned = []
    for k in range(1, half):
        pairs = [(g, g // half * half + (g + k) % half) for g in range(grids)]
        turned.append(lax.ppermute(t, "grid", pairs))
    far, cross, total = call(gather_kernel, [((32, 256), F32), (points, F32), (points, F32)], [VMEM] * 5)(
        t, *turned, off
    )
    far_in = lax.ppermute(far, "dom", pairs_off)
    cross_in = lax.ppermute(cross, ("grid", "dom"), pairs_cross)
    flip_in = lax.ppermute(total, "grid", pairs_flip)
    same_tail = lax.ppermute(tail, "dom", pairs_same)
    (acc,) = call(
        near_kernel,
        [(shape, F32)],
        [VMEM] * 3 + [SMEM] * 3,
        scratch=[VMEM(row, F32)],
        aliases={0: 0},
    )(acc, zones, same_head, *numbers_in)
    out, kept = call(
        change_kernel,
        [(shape, F32), (rest, F32)],
        [VMEM] * 9 + [SMEM] * 2,
        scratch=[
            VMEM((1024, LANES), F32),
            VMEM((1024, 256), F32),
            VMEM((8, MORE), F32),
            VMEM(row, F32),
            pltpu.SemaphoreType.DMA((8,)),
        ],
        space=pltpu.HBM,
    )(acc, own, total, far_in, cross_in, flip_in, table, zones, same_head, diffusion, courant)
    (out,) = call(
        last_kernel,
        [(shape, F32)],
        [VMEM] * 2 + [SMEM] * 2 + [pltpu.HBM],
        scratch=[VMEM(rest, F32), pltpu.SemaphoreType.DMA((PARTS,))],
        aliases={4: 0},
        space=pltpu.HBM,
    )(kept, same_tail, diffusion, courant, out)
    return out[None]


def solution(mesh):
    placed = (P("grid", "dom", None, None), P("grid", None), P("grid"), P(), P())
    return jax.shard_map(whole, mesh=mesh, in_specs=placed, out_specs=P("grid", "dom", None, None), check_vma=False)
```
